32 devices in a mesh: blk: 4 (over y, x), dom: 8 (over z, core).
Axes of the slice: x: 2, y: 2, z: 4, core: 2. Of those that a mesh axis runs over, the one named last changes fastest.
Arguments:
- orbitals: float32 [4, 64, 256, 256], P('blk', 'dom'), may hold values from -7 to 7
- dielectric: float32 [64, 256, 256], P('dom'), may hold values from 1 to 10
Outputs:
- exchange: float32 [4, 64, 256, 256], P('blk', 'dom')
The draws below stay inside these ranges and needn't reach their ends.
All inputs are finite; a program needn't handle non-finite values.
Results may differ from the reference program's by a relative error of at most 0.0001.
Values sent between devices are 32-bit elements; how exact they have to be, the bound alone decides.
No kernel may reach another device: no remote copies, remote signals or barrier semaphores. Data moves between devices by JAX's collectives and lax.ppermute only.
A program may use at most 128 MiB of HBM per device.

```python
import math
import jax
import jax.numpy as jnp
from jax import lax

NY = 256
NZ = 256
ITERS = 3
ORBS = 4
NX = 64


def draw_orbitals(key, part):
    fraction = jnp.arange(NX, dtype=jnp.float32) / max(NX - 1, 1)
    fraction = fraction.reshape(1, NX, 1, 1)
    pattern = jnp.clip(jax.random.normal(key, (ORBS, NX, NY, NZ), jnp.float32), -4.0, 4.0)
    envelope = jnp.power(3.0, fraction - 0.5)
    return (pattern * envelope).astype(jnp.float32)


def levels(rng, dims, cuts, least, high):
    level = 1.0
    for axis_at, shards_of in cuts:
        heights = jax.random.uniform(jax.random.fold_in(jax.random.fold_in(rng, 6), axis_at), (shards_of,), jnp.float32, least / len(cuts), high / len(cuts))
        level = level * jnp.repeat(jnp.exp(heights), dims[axis_at] // shards_of).reshape((-1,) + (1,) * (len(dims) - 1 - axis_at))
    return level


def setup_inputs(seed: int = 0) -> dict:
    arg_keys = jax.random.split(jax.random.key(seed), 3)
    orbitals = draw_orbitals(jax.random.fold_in(arg_keys[2], 71), 0)
    dielectric = jnp.clip(jnp.exp(math.log(10.0) - 2.3025851 * jax.random.uniform(arg_keys[1], (NX, NY, NZ), jnp.float32) ** levels(arg_keys[1], (NX, NY, NZ), ((0, 8),), -0.2, 0.2)), 1.0, 10.0)
    return {"orbitals": orbitals, "dielectric": dielectric}


FOUR_PI = 4.0 * math.pi


def face_weights(eps_pad):
    center = eps_pad[1:-1, 1:-1, 1:-1]
    return ((center + eps_pad[2:, 1:-1, 1:-1]) * 0.5,
            (center + eps_pad[:-2, 1:-1, 1:-1]) * 0.5,
            (center + eps_pad[1:-1, 2:, 1:-1]) * 0.5,
            (center + eps_pad[1:-1, :-2, 1:-1]) * 0.5,
            (center + eps_pad[1:-1, 1:-1, 2:]) * 0.5,
            (center + eps_pad[1:-1, 1:-1, :-2]) * 0.5)


def apply_operator(padded, weights):
    center = padded[:, 1:-1, 1:-1, 1:-1]
    result = weights[0] * (center - padded[:, 2:, 1:-1, 1:-1])
    result = result + weights[1] * (center - padded[:, :-2, 1:-1, 1:-1])
    result = result + weights[2] * (center - padded[:, 1:-1, 2:, 1:-1])
    result = result + weights[3] * (center - padded[:, 1:-1, :-2, 1:-1])
    result = result + weights[4] * (center - padded[:, 1:-1, 1:-1, 2:])
    result = result + weights[5] * (center - padded[:, 1:-1, 1:-1, :-2])
    return result


def inner_sum(first, second):
    return jnp.sum(first * second, axis=(1, 2, 3), keepdims=True)


def conjugate(right_side, weights):
    solution = jnp.zeros_like(right_side)
    residual = right_side
    direction = right_side
    norm_now = inner_sum(residual, residual)
    for iteration in range(ITERS):
        padded = jnp.pad(direction, ((0, 0), (1, 1), (1, 1), (1, 1)))
        applied = apply_operator(padded, weights)
        step_length = norm_now / inner_sum(direction, applied)
        solution = solution + step_length * direction
        residual = residual - step_length * applied
        norm_next = inner_sum(residual, residual)
        direction = residual + (norm_next / norm_now) * direction
        norm_now = norm_next
    return solution


def reference(orbitals, dielectric):
    weights = face_weights(jnp.pad(dielectric, 1))
    left_orbital = jnp.roll(orbitals, 1, axis=0)
    density = FOUR_PI * orbitals * left_orbital
    potential = lax.map(lambda single: conjugate(single[None], weights)[0], density)
    returned = jnp.roll(potential * orbitals, -1, axis=0)
    return -(potential * left_orbital + returned)
```

```python
import functools
import math

import jax
import jax.numpy as jnp
from jax import lax
from jax.experimental import pallas as pl
from jax.experimental.pallas import tpu as pltpu
from jax.sharding import PartitionSpec as P

FOUR_PI = 4.0 * math.pi
TILE = 8
LEFT = 2
RIGHT = 3
MOMENTS = 6
VMEM = pl.BlockSpec(memory_space=pltpu.VMEM)
SMEM = pl.BlockSpec(memory_space=pltpu.SMEM)


def roles(rows, window):
    odd = lax.rem(lax.axis_index("blk"), 2)
    upper = rows - window
    return (1 - odd) * upper, odd * upper


def edges():
    at = lax.axis_index("dom")
    last = lax.axis_size("dom") - 1
    return jnp.minimum(at, 1), jnp.minimum(last - at, 1)


def tile_rows(tile):
    return slice(tile * TILE, (tile + 1) * TILE)


def window_rows(start, tile):
    return pl.ds(pl.multiple_of(start + tile * TILE, TILE), TILE)


def next_lane(value):
    return pltpu.roll(value, value.shape[1] - 1, 1)


def prev_lane(value):
    return pltpu.roll(value, 1, 1)


def next_row(value):
    return pltpu.roll(value, TILE - 1, 0)


def prev_row(value):
    return pltpu.roll(value, 1, 0)


def build_weights(start, rows, layers, eps, eps_left, eps_right, half, wx, wy, wz, edge):
    tiles = half.shape[1] // TILE
    lanes = half.shape[2]
    slots = half.shape[0]
    below, above = edges()
    for source, first, count in ((eps_left, 0, LEFT), (eps, LEFT, layers), (eps_right, LEFT + layers, slots - LEFT - layers)):

        def copy(layer, carry, source=source, first=first):
            for tile in range(tiles):
                half[first + layer, tile_rows(tile)] = source[layer, window_rows(start, tile)] * 0.5
            return carry

        lax.fori_loop(0, count, copy, 0)
    row = lax.broadcasted_iota(jnp.int32, (TILE, lanes), 0)
    lane = lax.broadcasted_iota(jnp.int32, (TILE, lanes), 1)
    last_row = row == TILE - 1
    lane_inside = jnp.where(lane == lanes - 1, 0.0, 1.0)
    lane_edge = jnp.where(lane == 0, 1.0, 0.0) + jnp.where(lane == lanes - 1, 1.0, 0.0)
    at_low = jnp.where(start == 0, 1.0, 0.0)
    at_high = jnp.where(start + tiles * TILE == rows, 1.0, 0.0)
    low_edge = jnp.where(row == 0, at_low, 0.0)
    high_edge = jnp.where(last_row, at_high, 0.0)

    def one(slot, carry):
        x_open = jnp.where(slot == LEFT - 1, below, jnp.where(slot == LEFT + layers - 1, above, 1)).astype(jnp.float32)
        x_edge = jnp.where(slot == LEFT, 1 - below, 0) + jnp.where(slot == LEFT + layers - 1, 1 - above, 0)
        x_edge = x_edge.astype(jnp.float32)
        here = half[slot, tile_rows(0)]
        down = next_row(here)
        for tile in range(tiles):
            wx[slot, tile_rows(tile)] = (here + half[slot + 1, tile_rows(tile)]) * x_open
            wz[slot, tile_rows(tile)] = (here + next_lane(here)) * lane_inside
            border = lane_edge + x_edge
            if tile == 0:
                border = border + low_edge
            if tile == tiles - 1:
                border = border + high_edge
            edge[slot, tile_rows(tile)] = here * border
            if tile < tiles - 1:
                after = half[slot, tile_rows(tile + 1)]
                after_down = next_row(after)
                wy[slot, tile_rows(tile)] = here + jnp.where(last_row, after_down, down)
                here, down = after, after_down
            else:
                wy[slot, tile_rows(tile)] = jnp.where(last_row, 0.0, here + down)
        return carry

    lax.fori_loop(0, slots - 1, one, 0)


def flux_x(field, pair, slot, tile, wx):
    return wx[slot, tile_rows(tile)] * (field[pair, slot + 1, tile_rows(tile)] - field[pair, slot, tile_rows(tile)])


def sweep(field, pairs, first, stop, weights, carried, visit, finish=None):
    wx, wy, wz, edge = weights
    tiles = wy.shape[1] // TILE
    lanes = wy.shape[2]
    row = lax.broadcasted_iota(jnp.int32, (TILE, lanes), 0)
    first_row = row == 0
    last_row = row == TILE - 1
    for pair in range(pairs):
        for tile in range(tiles):
            carried[pair, tile_rows(tile)] = flux_x(field, pair, first - 1, tile, wx)

    def one(slot, carry):
        for pair in range(pairs):
            here = field[pair, slot, tile_rows(0)]
            down = next_row(here)
            came = jnp.zeros_like(here)
            for tile in range(tiles):
                rows = tile_rows(tile)
                along_x = wx[slot, rows] * (field[pair, slot + 1, rows] - here)
                from_x = carried[pair, rows]
                carried[pair, rows] = along_x
                along_z = wz[slot, rows] * (next_lane(here) - here)
                if tile < tiles - 1:
                    after = field[pair, slot, tile_rows(tile + 1)]
                    after_down = next_row(after)
                    below = jnp.where(last_row, after_down, down)
                else:
                    after, after_down, below = here, down, down
                along_y = wy[slot, rows] * (below - here)
                moved = prev_row(along_y)
                from_y = jnp.where(first_row, came, moved)
                came = moved
                result = ((from_x - along_x) + (from_y - along_y)) + ((prev_lane(along_z) - along_z) + edge[slot, rows] * here)
                visit(pair, slot, tile, here, result)
                here, down = after, after_down
            if finish is not None:
                finish(pair)
        return carry

    lax.fori_loop(first, stop, one, 0)


class Sums:
    def __init__(self, totals, tiles, shares):
        self.totals, self.tiles, self.shares = totals, tiles, shares
        self.held = {}

    def add(self, index, tile, value):
        if tile == 0:
            value = value * self.shares[0]
        if tile == self.tiles - 1:
            value = value * self.shares[1]
        self.held[index] = self.held[index] + value if index in self.held else value

    def flush(self, pair):
        for index, value in self.held.items():
            self.totals[pair, index] = self.totals[pair, index] + value
        self.held = {}


def moments_kernel(pairs, chunks, *refs):
    orbital, eps, eps_left, eps_right = refs[:4]
    refs = refs[4:]
    arrived = [refs[p * len(chunks) : (p + 1) * len(chunks)] for p in range(pairs)]
    refs = refs[pairs * len(chunks) :]
    halos = [refs[2 * p : 2 * p + 2] for p in range(pairs)]
    refs = refs[2 * pairs :]
    sums, basis, half, wx, wy, wz, edge, field, first, second, carried, totals = refs
    layers, rows, lanes = orbital.shape
    window = half.shape[1]
    tiles = window // TILE
    start, _ = roles(rows, window)
    weights = (wx, wy, wz, edge)
    build_weights(start, rows, layers, eps, eps_left, eps_right, half, *weights)
    low = jnp.where(start == 0, 1.0, 0.0)
    own = Sums(totals, tiles, (low, 1.0 - low))
    own_tile = jnp.where(start == 0, 0, 1)
    totals[...] = jnp.zeros_like(totals)
    for pair in range(pairs):
        left, right = halos[pair]
        field[pair, 0:LEFT] = left[...]
        field[pair, LEFT + layers :] = right[...]
        for part, (begin, end) in zip(arrived[pair], chunks):

            def one(layer, carry, part=part, begin=begin, pair=pair):
                for tile in range(tiles):
                    value = (FOUR_PI * orbital[layer, window_rows(start, tile)]) * part[layer - begin, tile_rows(tile)]
                    field[pair, LEFT + layer, tile_rows(tile)] = value
                    own.add(0, tile, value * value)
                own.flush(pair)
                return carry

            lax.fori_loop(begin, end, one, 0)

    def keep_first(pair, slot, tile, value, result):
        first[pair, slot, tile_rows(tile)] = result

    def sum_first(pair, slot, tile, value, result):
        first[pair, slot, tile_rows(tile)] = result
        own.add(1, tile, value * result)
        own.add(2, tile, result * result)

    def keep_second(pair, slot, tile, value, result):
        second[pair, slot, tile_rows(tile)] = result

    def sum_second(pair, slot, tile, value, result):
        second[pair, slot, tile_rows(tile)] = result
        own.add(3, tile, value * result)
        own.add(4, tile, result * result)

    def sum_third(pair, slot, tile, value, result):
        own.add(5, tile, value * result)

    begin, end = LEFT, LEFT + layers
    sweep(field, pairs, begin - 1, begin, weights, carried, keep_first)
    sweep(field, pairs, begin, end, weights, carried, sum_first, own.flush)
    sweep(field, pairs, end, end + 2, weights, carried, keep_first)
    sweep(first, pairs, begin, end, weights, carried, sum_second, own.flush)
    sweep(first, pairs, end, end + 1, weights, carried, keep_second)
    face_sums(second, pairs, begin, end, weights, own)
    lane = lax.broadcasted_iota(jnp.int32, (1, sums.shape[1]), 1)
    line = jnp.zeros((1, sums.shape[1]), jnp.float32)
    for pair in range(pairs):
        for index in range(MOMENTS):
            total = jnp.sum(totals[pair, index])
            line = line + jnp.where(lane == pair * MOMENTS + index, total, 0.0)
    sums[...] = line

    def store(layer, carry):
        for pair in range(pairs):
            for order, source in enumerate((field, first, second)):
                for tile in range(tiles - 1):
                    basis[pair, order, layer, tile_rows(tile)] = source[pair, LEFT + layer, window_rows(own_tile * TILE, tile)]
        return carry

    lax.fori_loop(0, layers, store, 0)


def face_sums(field, pairs, begin, end, weights, own):
    wx, wy, wz, edge = weights
    tiles = wy.shape[1] // TILE
    lanes = wy.shape[2]
    row = lax.broadcasted_iota(jnp.int32, (TILE, lanes), 0)
    last_row = row == TILE - 1

    def one(slot, carry):
        for pair in range(pairs):
            here = field[pair, slot, tile_rows(0)]
            down = next_row(here)
            for tile in range(tiles):
                rows = tile_rows(tile)
                step_x = field[pair, slot + 1, rows] - here
                step_z = next_lane(here) - here
                if tile < tiles - 1:
                    after = field[pair, slot, tile_rows(tile + 1)]
                    after_down = next_row(after)
                    below = jnp.where(last_row, after_down, down)
                else:
                    after, after_down, below = here, down, down
                step_y = below - here
                value = (wx[slot, rows] * step_x * step_x + wy[slot, rows] * step_y * step_y) + (
                    wz[slot, rows] * step_z * step_z + edge[slot, rows] * here * here
                )
                own.add(5, tile, value)
                here, down = after, after_down
            own.flush(pair)
        return carry

    lax.fori_loop(begin, end, one, 0)


def first_output_kernel(pairs, chunks, scalars, basis, *refs):
    arrived = [refs[p * len(chunks) : (p + 1) * len(chunks)] for p in range(pairs)]
    out = refs[-1]
    layers, own_rows, _ = out.shape
    window = arrived[0][0].shape[1]
    low_window = lax.rem(lax.axis_index("blk"), 2)
    skip = (1 - low_window) * TILE
    for index, (begin, end) in enumerate(chunks):

        def one(layer, carry, index=index, begin=begin):
            for tile in range(own_rows // TILE):
                rows = tile_rows(tile)
                total = None
                for pair in range(pairs):
                    potential = (
                        scalars[pair, 0] * basis[pair, 0, layer, rows]
                        + scalars[pair, 1] * basis[pair, 1, layer, rows]
                        + scalars[pair, 2] * basis[pair, 2, layer, rows]
                    )
                    term = potential * arrived[pair][index][layer - begin, window_rows(skip, tile)]
                    total = term if total is None else total + term
                out[layer, rows] = -total
            return carry

        lax.fori_loop(begin, end, one, 0)


def second_output_kernel(pairs, chunks, late_chunks, scalars, orbital, eps, eps_left, eps_right, other, *refs):
    n = len(chunks)
    early = [refs[p * n : (p + 1) * n] for p in range(pairs)]
    refs = refs[pairs * n :]
    n = len(late_chunks)
    late = [refs[p * n : (p + 1) * n] for p in range(pairs)]
    refs = refs[pairs * n :]
    halos = [refs[2 * p : 2 * p + 2] for p in range(pairs)]
    refs = refs[2 * pairs :]
    out, half, wx, wy, wz, edge, whole, field, first, carried = refs
    layers, rows, lanes = orbital.shape
    window = half.shape[1]
    tiles = window // TILE
    late_rows = late[0][0].shape[1]
    shared = window - late_rows
    before, start = roles(rows, window)
    weights = (wx, wy, wz, edge)
    build_weights(start, rows, layers, eps, eps_left, eps_right, half, *weights)
    low = jnp.where(start == 0, 1, 0)
    late_at = (1 - low) * shared
    early_at = low * late_rows
    early_from = (1 - low) * (window - shared)
    for pair in range(pairs):
        left, right = halos[pair]
        field[pair, 0:LEFT] = left[...]
        field[pair, LEFT + layers :] = right[...]
        for part, (begin, end) in zip(early[pair], chunks):

            def take_early(layer, carry, part=part, begin=begin, pair=pair):
                for tile in range(shared // TILE):
                    whole[pair, layer, window_rows(early_at, tile)] = part[layer - begin, window_rows(early_from, tile)]
                return carry

            lax.fori_loop(begin, end, take_early, 0)
        for part, (begin, end) in zip(late[pair], late_chunks):

            def take_late(layer, carry, part=part, begin=begin, pair=pair):
                for tile in range(late_rows // TILE):
                    whole[pair, layer, window_rows(late_at, tile)] = part[layer - begin, tile_rows(tile)]
                return carry

            lax.fori_loop(begin, end, take_late, 0)

        def density(layer, carry, pair=pair):
            for tile in range(tiles):
                value = (FOUR_PI * orbital[layer, window_rows(start, tile)]) * whole[pair, layer, tile_rows(tile)]
                field[pair, LEFT + layer, tile_rows(tile)] = value
            return carry

        lax.fori_loop(0, layers, density, 0)

    def inner(pair, slot, tile, value, result):
        first[pair, slot, tile_rows(tile)] = scalars[pair, 1] * value + scalars[pair, 2] * result

    begin, end = LEFT, LEFT + layers
    sweep(field, pairs, begin - 1, end + 1, weights, carried, inner)

    def outer(pair, slot, tile, value, result):
        rows_ = tile_rows(tile)
        potential = scalars[pair, 0] * field[pair, slot, rows_] + result
        field[pair, slot, rows_] = potential * whole[pair, slot - LEFT, rows_]

    sweep(first, pairs, begin, end, weights, carried, outer)
    own_rows = rows // 2
    own_from = (1 - low) * TILE
    own_at = (1 - low) * own_rows
    other_at = low * own_rows

    def store(layer, carry):
        for tile in range(own_rows // TILE):
            total = field[0, LEFT + layer, window_rows(own_from, tile)]
            for pair in range(1, pairs):
                total = total + field[pair, LEFT + layer, window_rows(own_from, tile)]
            out[layer, window_rows(own_at, tile)] = -total
            out[layer, window_rows(other_at, tile)] = other[layer, tile_rows(tile)]
        return carry

    lax.fori_loop(0, layers, store, 0)


def call(kernel, out_shape, scratch, args, name, in_specs=None, work=4_000_000):
    return pl.pallas_call(
        kernel,
        out_shape=out_shape,
        in_specs=in_specs or [VMEM] * len(args),
        out_specs=jax.tree.map(lambda _: VMEM, out_shape),
        scratch_shapes=scratch,
        compiler_params=pltpu.CompilerParams(vmem_limit_bytes=48 << 20),
        cost_estimate=pl.CostEstimate(flops=work, bytes_accessed=work, transcendentals=0),
        name=name,
    )(*args)


def f32(*shape):
    return jax.ShapeDtypeStruct(shape, jnp.float32)


def buffer(*shape):
    return pltpu.VMEM(shape, jnp.float32)


def weight_scratch(slots, window, lanes):
    return [buffer(slots, window, lanes)] + [buffer(slots - 1, window, lanes)] * 4


def coefficients(moments):
    def inner(left, right, power):
        total = 0.0
        for i, p in enumerate(left):
            for j, q in enumerate(right):
                total = total + (p * q) * moments[..., i + j + power]
        return total

    one = jnp.ones_like(moments[..., 0])
    answer = [0.0 * one] * 3
    residual, direction = [one], [one]
    norm = moments[..., 0]
    for iteration in range(3):
        step = norm / inner(direction, direction, 1)
        answer = [answer[i] + step * direction[i] if i < len(direction) else answer[i] for i in range(3)]
        if iteration == 2:
            break
        applied = [0.0] + [step * p for p in direction]
        residual = residual + [0.0 * one]
        residual = [r - q for r, q in zip(residual, applied)]
        norm_next = inner(residual, residual, 0)
        ratio = norm_next / norm
        direction = direction + [0.0 * one]
        direction = [r + ratio * p for r, p in zip(residual, direction)]
        norm = norm_next
    return jnp.stack(answer, axis=-1)


def per_device(orbitals, dielectric):
    orbital = orbitals[0]
    layers, rows, lanes = orbital.shape
    blks, doms = lax.axis_size("blk"), lax.axis_size("dom")
    own_rows = rows // 2
    window = own_rows + TILE
    rest = rows - window
    slots = LEFT + layers + RIGHT
    start, other_start = roles(rows, window)
    odd = lax.rem(lax.axis_index("blk"), 2)
    pair_up = [(i, i ^ 1) for i in range(blks)]
    forward = [(i, (i + 2 - 4 * (i % 2)) % blks) for i in range(blks)]
    to_above = [(i, i + 1) for i in range(doms - 1)]
    to_below = [(i + 1, i) for i in range(doms - 1)]

    def halo(first, last):
        return lax.ppermute(last, "dom", to_above), lax.ppermute(first, "dom", to_below)

    chunks = ((0, 3), (3, layers - 2), (layers - 2, layers))
    send_first = lax.dynamic_slice_in_dim(orbital, other_start, window, axis=1)
    send_second = lax.dynamic_slice_in_dim(orbital, (1 - odd) * window, rest, axis=1)

    eps_left, eps_right = halo(dielectric[:RIGHT], dielectric[layers - LEFT :])
    near = [lax.ppermute(send_first[a:b], "blk", pair_up) for a, b in chunks]
    far = [lax.ppermute(part, "blk", forward) for part in near]
    late_near = [lax.ppermute(send_second[a:b], "blk", pair_up) for a, b in chunks]
    late_far = [lax.ppermute(part, "blk", forward) for part in late_near]

    mine = lax.dynamic_slice_in_dim(orbital, start, window, axis=1)

    def early_halo(parts):
        return halo(FOUR_PI * mine[:RIGHT] * parts[0], FOUR_PI * mine[layers - LEFT :] * parts[2])

    halos = [*early_halo(near), *early_halo(far)]
    weights = weight_scratch(slots, window, lanes)
    sums, basis = call(
        functools.partial(moments_kernel, 2, chunks),
        (f32(1, 128), f32(2, 3, layers, own_rows, lanes)),
        weights
        + [
            buffer(2, slots, window, lanes),
            buffer(2, slots - 1, window, lanes),
            buffer(2, slots - 2, window, lanes),
            buffer(2, window, lanes),
            buffer(2, MOMENTS, TILE, lanes),
        ],
        [orbital, dielectric, eps_left, eps_right, *near, *far, *halos],
        "moments",
    )
    every = lax.all_to_all(jnp.broadcast_to(sums[None], (blks * doms, 1, 128)), ("blk", "dom"), 0, 0, tiled=True)
    every = jnp.sum(every.reshape(blks, doms, 128), axis=1)
    near_sums = every[:, :MOMENTS]
    far_sums = every[:, MOMENTS : 2 * MOMENTS]
    near_sums = near_sums + near_sums[jnp.array([i ^ 1 for i in range(blks)])]
    far_sums = far_sums + far_sums[jnp.array([(i - 1 + 2 * (i % 2)) % blks for i in range(blks)])]
    scalars = coefficients(jnp.stack([near_sums, far_sums], axis=1))
    scalars = lax.dynamic_index_in_dim(scalars, lax.axis_index("blk"), 0, keepdims=False)

    first_half = call(
        functools.partial(first_output_kernel, 2, chunks),
        f32(layers, own_rows, lanes),
        [],
        [scalars, basis, *near, *far],
        "first_output",
        [SMEM] + [VMEM] * (1 + 2 * len(chunks)),
    )

    mine_late = lax.dynamic_slice_in_dim(orbital, (odd * window), rest, axis=1)
    mine_shared = lax.dynamic_slice_in_dim(orbital, rest, window - rest, axis=1)

    def late_halo(parts, early_parts):
        def product(layer_slice, part, early_part):
            late = FOUR_PI * mine_late[layer_slice] * part
            seam = lax.dynamic_slice_in_dim(early_part, odd * rest, window - rest, axis=1)
            seam = FOUR_PI * mine_shared[layer_slice] * seam
            return jnp.where(odd == 1, jnp.concatenate([seam, late], 1), jnp.concatenate([late, seam], 1))

        low = product(slice(0, 2), parts[0][:2], early_parts[0][:2])
        high = product(slice(layers - LEFT, layers), parts[2], early_parts[2])
        return halo(low, high)

    late_halos = [*late_halo(late_near, near), *late_halo(late_far, far)]
    slots = slots - 1
    out = call(
        functools.partial(second_output_kernel, 2, chunks, chunks),
        f32(layers, rows, lanes),
        weight_scratch(slots, window, lanes)
        + [
            buffer(2, layers, window, lanes),
            buffer(2, slots, window, lanes),
            buffer(2, slots - 1, window, lanes),
            buffer(2, window, lanes),
        ],
        [scalars, orbital, dielectric, eps_left, eps_right, first_half, *near, *far, *late_near, *late_far, *late_halos],
        "second_output",
        [SMEM] + [VMEM] * (5 + 4 * len(chunks) + 4),
    )
    return out[None]


def solution(mesh):
    return jax.shard_map(
        per_device,
        mesh=mesh,
        in_specs=(P("blk", "dom", None, None), P("dom", None, None)),
        out_specs=P("blk", "dom", None, None),
        check_vma=False,
    )
```
